32 devices in a mesh: gx: 2 (over x), gy: 4 (over y, core), gz: 4 (over z).
Axes of the slice: x: 2, y: 2, z: 4, core: 2. Of those that a mesh axis runs over, the one named last changes fastest.
Arguments:
- residual: bfloat16 [2, 4, 4, 3, 256, 256], P('gx', 'gy', 'gz'), may hold values from -6 to 6
- face_basis: bfloat16 [2, 4, 4, 3, 256, 256], P('gx', 'gy', 'gz'), may hold values from -0.375 to 0.375
- factor: bfloat16 [2, 4, 4, 768, 768], P('gx', 'gy', 'gz'), may hold values from -0.21875 to 0.21875
- coarse_inv: bfloat16 [2, 4, 4, 768, 768], P('gx', 'gy', 'gz'), may hold values from -0.21875 to 0.21875
- item_owner: int32 [2, 4, 4, 24], P('gx', 'gy', 'gz'), may hold values from 0 to 3, as said below
Outputs:
- result: bfloat16 [2, 4, 4, 3, 256, 256], P('gx', 'gy', 'gz')
The draws below stay inside these ranges and needn't reach their ends.
Inputs may be any that keep to these rules, and one draw needn't show every extreme that they name: `item_owner`: within the groups of one subdomain, at most 12 name the same owner, and in every subdomain some owner is named exactly 12 times.
All inputs are finite; a program needn't handle non-finite values.
Results may differ from the reference program's by a relative error of at most 0.006.
Values may be sent and summed in bfloat16 or wider, within the bound.
No kernel may reach another device: no remote copies, remote signals or barrier semaphores. Data moves between devices by JAX's collectives and lax.ppermute only.
A program may use at most 64 MiB of HBM per device.

```python
import jax
import jax.numpy as jnp
from jax import lax

R = 256
FACE = 256
PF = 128
GROUP = 16
ITEMS = 24
SEND_CAP = 12
DF = 128
SOLVE = 768
CS = 768
N_GX = 2
N_GY = 4
N_GZ = 4


def draw_item_owner(key, part):
    slot_total = SEND_CAP * N_GZ
    key_popular, key_owner, key_slot, key_shuffle = jax.random.split(jax.random.fold_in(key, 17), 4)
    grid_shape = (N_GX, N_GY, N_GZ)
    popular = jax.random.randint(key_popular, (N_GX, N_GY, 1, N_GZ), 0, 4) == 0
    owner_score = jax.random.randint(key_owner, grid_shape + (N_GZ,), 0, 64) + jnp.where(popular, 0, 48)
    owner_index = jnp.arange(N_GZ, dtype=jnp.int32)
    owner_order = jnp.argsort(owner_score * N_GZ + owner_index, axis=-1, stable=True).astype(jnp.int32)
    slot_index = jnp.arange(slot_total, dtype=jnp.int32)
    slot_score = (jax.random.randint(key_slot, grid_shape + (slot_total,), 0, slot_total) + slot_index) * slot_total + slot_index
    slot_score = jnp.where(slot_index < SEND_CAP, slot_index - slot_total, slot_score)
    chosen = jnp.argsort(slot_score, axis=-1, stable=True)[..., :ITEMS].astype(jnp.int32)
    shuffle_score = jax.random.randint(key_shuffle, grid_shape + (ITEMS,), 0, 1 << 20) * ITEMS + jnp.arange(ITEMS, dtype=jnp.int32)
    shuffle = jnp.argsort(shuffle_score, axis=-1, stable=True).astype(jnp.int32)
    picked = jnp.take_along_axis(chosen, shuffle, axis=-1)
    bins = picked // SEND_CAP
    return jnp.take_along_axis(owner_order, bins, axis=-1).astype(jnp.int32)


def levels(key, dims, pieces, smallest, largest):
    def one(dim, shards_of):
        heights = jax.random.uniform(jax.random.fold_in(jax.random.fold_in(key, 6), dim), (shards_of,), jnp.float32, smallest / len(pieces), largest / len(pieces))
        return jnp.repeat(jnp.exp(heights), dims[dim] // shards_of).reshape((-1,) + (1,) * (len(dims) - dim - 1))

    factor_of = one(*pieces[0])
    for cut in pieces[1:]:
        factor_of = factor_of * one(*cut)
    return factor_of


def scatter_about(own_key, dims, scale, limit, pieces=(), kind=jnp.bfloat16):
    level = levels(own_key, dims, pieces, -0.22, 0.18) if pieces else 1.0
    entries = jax.random.normal(own_key, dims, jnp.float32) * scale * level
    return jnp.minimum(jnp.maximum(entries, -limit), limit).astype(kind)


def setup_inputs(seed: int = 0) -> dict:
    seeds = jax.random.split(jax.random.key(seed), 6)
    residual = scatter_about(seeds[0], (N_GX, N_GY, N_GZ, 3, FACE, R), 1.0, 6.0, ((0, 2), (1, 4), (2, 4)))
    face_basis = scatter_about(seeds[1], (N_GX, N_GY, N_GZ, 3, FACE, FACE), FACE ** -0.5, 0.375, ((0, 2), (1, 4), (2, 4)))
    factor = scatter_about(seeds[2], (N_GX, N_GY, N_GZ, SOLVE, SOLVE), SOLVE ** -0.5, 0.21875, ((0, 2), (1, 4), (2, 4)))
    coarse_inv = scatter_about(seeds[3], (N_GX, N_GY, N_GZ, CS, CS), CS ** -0.5, 0.21875, ((0, 2), (1, 4), (2, 4)))
    item_owner = draw_item_owner(jax.random.fold_in(seeds[5], 71), 0)
    return {"residual": residual, "face_basis": face_basis, "factor": factor, "coarse_inv": coarse_inv, "item_owner": item_owner}


def solve_twice(pair):
    matrix, vector = pair
    half_solve = lax.dot_general(matrix, vector, (((0,), (0,)), ((), ())), preferred_element_type=jnp.float32).astype(jnp.bfloat16)
    return jnp.dot(matrix, half_solve, preferred_element_type=jnp.float32).astype(jnp.bfloat16)


def coarse_apply(pair):
    matrix, vector = pair
    return lax.dot_general(matrix, vector, (((0,), (0,)), ((), ())), preferred_element_type=jnp.float32).astype(jnp.bfloat16)


def reference(residual, face_basis, factor, coarse_inv, item_owner):
    count = N_GX * N_GY * N_GZ
    transformed = jnp.einsum('xyzfac,xyzfar->xyzfcr', face_basis.astype(jnp.float32), residual.astype(jnp.float32))
    primal_items = transformed[:, :, :, :, :PF, :].astype(jnp.bfloat16).reshape(N_GX, N_GY, N_GZ, ITEMS, GROUP, R)
    dual_own = transformed[:, :, :, :, PF:, :].astype(jnp.bfloat16)
    dual_in = jnp.stack([jnp.roll(dual_own[:, :, :, 0], 1, axis=0), jnp.roll(dual_own[:, :, :, 1], 1, axis=1), jnp.roll(dual_own[:, :, :, 2], 1, axis=2)], axis=3)
    dual_load = (jnp.concatenate([dual_in, dual_own], axis=3) * 0.5).astype(jnp.bfloat16).reshape(count, SOLVE, R)
    solved = lax.map(solve_twice, (factor.reshape(count, SOLVE, SOLVE), dual_load)).reshape(N_GX, N_GY, N_GZ, 6, DF, R)
    lower_faces = solved[:, :, :, :3]
    upper_faces = solved[:, :, :, 3:]
    from_above = jnp.stack([jnp.roll(lower_faces[:, :, :, 0], -1, axis=0), jnp.roll(lower_faces[:, :, :, 1], -1, axis=1), jnp.roll(lower_faces[:, :, :, 2], -1, axis=2)], axis=3)
    dual_part = (0.5 * (upper_faces.astype(jnp.float32) + from_above.astype(jnp.float32))).astype(jnp.bfloat16)
    same_owner = item_owner[..., :, None] == item_owner[..., None, :]
    item_index = jnp.arange(ITEMS, dtype=jnp.int32)
    earlier = item_index[:, None] > item_index[None, :]
    slot_rank = jnp.sum((same_owner & earlier).astype(jnp.int32), axis=-1).astype(jnp.int32)
    gx_index = jnp.arange(N_GX, dtype=jnp.int32)[:, None, None, None]
    gy_index = jnp.arange(N_GY, dtype=jnp.int32)[None, :, None, None]
    gz_index = jnp.arange(N_GZ, dtype=jnp.int32)[None, None, :, None]
    holder = jnp.zeros((N_GX, N_GY, N_GZ, N_GZ, SEND_CAP, GROUP, R), jnp.bfloat16)
    holder = holder.at[gx_index, gy_index, item_owner, gz_index, slot_rank].set(primal_items)
    coarse_sol = lax.map(coarse_apply, (coarse_inv.reshape(count, CS, CS), holder.reshape(count, CS, R)))
    coarse_sol = coarse_sol.reshape(N_GX, N_GY, N_GZ, N_GZ, SEND_CAP, GROUP, R)
    primal_part = coarse_sol[gx_index, gy_index, item_owner, gz_index, slot_rank].reshape(N_GX, N_GY, N_GZ, 3, PF, R)
    combined = jnp.concatenate([primal_part, dual_part], axis=4)
    result = jnp.einsum('xyzfac,xyzfcr->xyzfar', face_basis.astype(jnp.float32), combined.astype(jnp.float32))
    return result.astype(jnp.bfloat16)
```

```python
import functools

import jax
import jax.numpy as jnp
from jax import lax
from jax.experimental import pallas as pl
from jax.experimental.pallas import tpu as pltpu
from jax.sharding import PartitionSpec as P

GROUP = 16
BF16 = jnp.bfloat16
F32 = jnp.float32
VMEM = pl.BlockSpec(memory_space=pltpu.VMEM)
SMEM = pl.BlockSpec(memory_space=pltpu.SMEM)


def dot_tn(a, b):
    return lax.dot_general(a, b, (((0,), (0,)), ((), ())), preferred_element_type=F32)


def dot_nn(a, b):
    return lax.dot_general(a, b, (((1,), (0,)), ((), ())), preferred_element_type=F32)


def call(kernel, outs, scratch, args, in_specs=None, flops=0, limit=12 << 20, name=None):
    nbytes = sum(a.size * a.dtype.itemsize for a in args)
    return pl.pallas_call(
        kernel,
        out_shape=outs,
        in_specs=in_specs or [VMEM] * len(args),
        out_specs=jax.tree.map(lambda _: VMEM, outs),
        scratch_shapes=scratch,
        compiler_params=pltpu.CompilerParams(vmem_limit_bytes=limit),
        cost_estimate=pl.CostEstimate(flops=flops, bytes_accessed=nbytes, transcendentals=0),
        name=name,
    )(*args)


def ranks(owner_ref, count_ref, n, items):
    for o in range(n):
        count_ref[o] = 0
    for i in range(items):
        o = owner_ref[i]
        r = count_ref[o]
        count_ref[o] = r + 1
        yield i, o, r


def pack_kernel(n, cap, pf, owner_ref, resid_ref, basis_ref, *refs):
    outs, dual_ref = refs[:n], refs[n]
    slots, count = refs[n + 1], refs[n + 2]
    faces = resid_ref.shape[0]
    per_face = pf // GROUP
    me = lax.axis_index("gz")
    slots[...] = jnp.zeros_like(slots)
    where = {}
    for i, o, r in ranks(owner_ref, count, n, faces * per_face):
        d = lax.rem(o - me + n, n)
        where[i] = d * cap + r
    for k in range(faces):
        t = dot_tn(basis_ref[k], resid_ref[k])
        primal = t[:pf].astype(BF16)
        for g in range(per_face):
            slots[where[k * per_face + g]] = primal[g * GROUP : (g + 1) * GROUP]
        dual = t[pf:].astype(BF16)
        dual_ref[k] = dual
        if k == faces - 1:
            outs[1][cap * GROUP :] = dual
    rows = cap * GROUP
    for d in range(n):
        outs[d][:rows] = slots[d * cap : (d + 1) * cap].reshape(rows, -1)


def coarse_kernel(n, rows, matrix_ref, *refs):
    recv, outs, vec, sol = refs[:n], refs[n : 2 * n], refs[2 * n], refs[2 * n + 1]
    me = lax.axis_index("gz")
    for d in range(n):
        c = lax.rem(me - d + n, n)
        vec[pl.ds(pl.multiple_of(c * rows, GROUP), rows)] = recv[d][:rows]
    sol[...] = dot_tn(matrix_ref[...], vec[...]).astype(BF16)
    for d in range(n):
        c = lax.rem(me + d, n)
        outs[d][...] = sol[pl.ds(pl.multiple_of(c * rows, GROUP), rows)]


def solve_kernel(rows, factor_ref, x_ref, y_ref, z_ref, own_ref, low_ref, high_ref, load):
    df = x_ref.shape[0]
    half = jnp.asarray(0.5, BF16)
    load[:df] = x_ref[...] * half
    load[df : 2 * df] = y_ref[...] * half
    load[2 * df : 3 * df] = z_ref[rows:] * half
    for k in range(3):
        load[(3 + k) * df : (4 + k) * df] = own_ref[k] * half
    h = dot_tn(factor_ref[...], load[...]).astype(BF16)
    s = dot_nn(factor_ref[...], h).astype(BF16)
    for k in range(3):
        low_ref[k] = s[k * df : (k + 1) * df]
        high_ref[k] = s[(3 + k) * df : (4 + k) * df]


def final_kernel(n, cap, pf, owner_ref, basis_ref, x_ref, y_ref, z_ref, high_ref, *refs):
    recv, out_ref, slots, comb, count = refs[:n], refs[n], refs[n + 1], refs[n + 2], refs[n + 3]
    me = lax.axis_index("gz")
    faces = basis_ref.shape[0]
    per_face = pf // GROUP
    for d in range(n):
        slots[d * cap : (d + 1) * cap] = recv[d][...].reshape(cap, GROUP, -1)
    for i, o, r in ranks(owner_ref, count, n, faces * per_face):
        d = lax.rem(me - o + n, n)
        k, g = divmod(i, per_face)
        comb[k, g * GROUP : (g + 1) * GROUP] = slots[d * cap + r]
    for k, above in enumerate((x_ref, y_ref, z_ref)):
        mean = 0.5 * (high_ref[k].astype(F32) + above[...].astype(F32))
        comb[k, pf:] = mean.astype(BF16)
    for k in range(faces):
        out_ref[k] = dot_nn(basis_ref[k], comb[k]).astype(BF16)


def shift(block, axis, distance):
    n = lax.axis_size(axis)
    return lax.ppermute(block, axis, [(i, (i + distance) % n) for i in range(n)])


def body(residual, face_basis, factor, coarse_inv, item_owner):
    resid, basis = residual[0, 0, 0], face_basis[0, 0, 0]
    matrix, inverse = factor[0, 0, 0], coarse_inv[0, 0, 0]
    owners = item_owner[0, 0, 0]
    faces, _, cols = resid.shape
    items = owners.shape[0]
    pf = items * GROUP // faces
    df = resid.shape[1] - pf
    n = lax.axis_size("gz")
    cap = inverse.shape[0] // (n * GROUP)
    rows = cap * GROUP
    flat = lambda r: jax.ShapeDtypeStruct((r, cols), BF16)
    cube = lambda r: jax.ShapeDtypeStruct((faces, r, cols), BF16)

    packed = call(
        functools.partial(pack_kernel, n, cap, pf),
        [flat(rows + df if d == 1 else rows) for d in range(n)] + [cube(df)],
        [pltpu.VMEM((n * cap, GROUP, cols), BF16), pltpu.SMEM((n,), jnp.int32)],
        (owners, resid, basis),
        [SMEM, VMEM, VMEM],
        name="pack",
    )
    sends, dual_own = packed[:n], packed[n]
    recv = [sends[0]] + [shift(sends[d], "gz", d) for d in range(1, n)]
    from_x = shift(dual_own[0], "gx", 1)
    from_y = shift(dual_own[1], "gy", 1)
    low, high = call(
        functools.partial(solve_kernel, rows),
        [cube(df), cube(df)],
        [pltpu.VMEM((matrix.shape[0], cols), BF16)],
        (matrix, from_x, from_y, recv[1], dual_own),
        name="solve",
    )
    back_x = shift(low[0], "gx", -1)
    back_y = shift(low[1], "gy", -1)
    answers = call(
        functools.partial(coarse_kernel, n, rows),
        [flat(rows)] * n,
        [pltpu.VMEM((inverse.shape[0], cols), BF16)] * 2,
        (inverse, *recv),
        name="coarse",
    )
    back = [answers[0]] + [shift(answers[d], "gz", d) for d in range(1, n)]
    back_z = shift(low[2], "gz", -1)
    result = call(
        functools.partial(final_kernel, n, cap, pf),
        cube(pf + df),
        [
            pltpu.VMEM((n * cap, GROUP, cols), BF16),
            pltpu.VMEM((faces, pf + df, cols), BF16),
            pltpu.SMEM((n,), jnp.int32),
        ],
        (owners, basis, back_x, back_y, back_z, high, *back),
        [SMEM] + [VMEM] * (5 + n),
        name="final",
    )
    return result[None, None, None]


def solution(mesh):
    in_specs = (
        P("gx", "gy", "gz", None, None, None),
        P("gx", "gy", "gz", None, None, None),
        P("gx", "gy", "gz", None, None),
        P("gx", "gy", "gz", None, None),
        P("gx", "gy", "gz", None),
    )
    out_specs = P("gx", "gy", "gz", None, None, None)
    return jax.shard_map(body, mesh=mesh, in_specs=in_specs, out_specs=out_specs, check_vma=False)
```
